32 devices in a mesh: groups: 2 (over x), pts: 8 (over z, y), sn: 2 (over core).
Axes of the slice: x: 2, y: 2, z: 4, core: 2. Of those that a mesh axis runs over, the one named last changes fastest.
Arguments:
- point_features: bfloat16 [131072, 192], P(('groups', 'pts', 'sn')), parts along dimension 0, may hold values from -6 to 6
- point_positions: float32 [3, 131072], P(None, ('groups', 'pts', 'sn')), parts along dimension 1, may hold values from 0 to 1
- sn_positions: float32 [3, 32768], P(None, ('groups', 'pts', 'sn')), parts along dimension 1, may hold values from 0 to 1
- latent_queries: bfloat16 [512, 192], replicated, may hold values from -500 to 500
- target_block: int32 [256], P('groups'), parts along dimension 0, may hold values from 0 to 127, as said below
- target_links: int32 [256, 3], P(('groups', 'pts', 'sn')), parts along dimension 0, may hold values from 0 to 31
- target_count: int32 [32], P('groups'), parts along dimension 0, may hold values from 6 to 8, as said below
- block_slot: int32 [256], P('groups'), parts along dimension 0, may hold values from 0 to 127, as said below
- w_in: bfloat16 [192, 192], replicated, may hold values from -0.4375 to 0.4375
- w_mid: bfloat16 [192, 192], replicated, may hold values from -0.4375 to 0.4375
- w_post: bfloat16 [192, 192], replicated, may hold values from -1.25 to 1.25
- w_key: bfloat16 [192, 192], replicated, may hold values from -0.4375 to 0.4375
- w_value: bfloat16 [192, 192], replicated, may hold values from -0.4375 to 0.4375
- w_out: bfloat16 [192, 192], replicated, may hold values from -0.4375 to 0.4375
- out_gain: float32 [192], replicated, may hold values from 0.1 to 1.9
Outputs:
- supernode_features: bfloat16 [32768, 192], P(('groups', 'pts', 'sn')), parts along dimension 0
- latent_out: bfloat16 [1024, 192], P(('groups', 'pts', 'sn')), parts along dimension 0
The draws below stay inside these ranges and needn't reach their ends.
There are 2 independent parts, one for each index of `groups`. The reference program is written for one: setup_inputs(seed, part) draws one part's arguments, and reference() takes and returns one part's arrays. A program takes and returns all parts, laid end to end along the dimension named above; an argument that names none is the same for every part. Nothing has to cross between parts.
Inputs may be any that keep to these rules, and one draw needn't show every extreme that they name: `target_block`: the 8 targets of one region name blocks of distinct owners, the owner of a block being its slot divided by 8; one owner, the same for all regions, holds the first target of every region. `target_count`: the live targets of a region are its first ones; some region has all 8 live. `block_slot`: A permutation.
All inputs are finite; a program needn't handle non-finite values.
Results may differ from the reference program's by a relative error of at most 0.012.
The reference program's roundings to bfloat16 on the way count: a program that leaves them out, or rounds other values in their place, can miss the bound.
Values may be sent and summed in bfloat16 or wider, within the bound.
A program may use at most 256 MiB of HBM per device.

```python
import jax
import jax.numpy as jnp
from jax import lax

D = 192
HEADS = 3
BLOCK = 128
LINKS = 3
PB_DEV = 32
SNB_DEV = 8
LATENTS = 512
KEY_BLOCK = 512
OWNERS = 16
TARGETS_DEV = 8
SN_BLOCKS = 128
SUPERNODES = 16384
POINTS = 65536
N_PTS = 8
N_SN = 2


def graph_tables(key):
    slot_of_block = jax.random.permutation(jax.random.fold_in(key, 11), SN_BLOCKS).astype(jnp.int32)
    block_of_slot = jnp.zeros((SN_BLOCKS,), jnp.int32).at[slot_of_block].set(jnp.arange(SN_BLOCKS, dtype=jnp.int32))
    hot_owner = jax.random.randint(jax.random.fold_in(key, 12), (), 0, OWNERS)
    row_keys = jax.random.split(jax.random.fold_in(key, 13), OWNERS)
    others = jax.vmap(lambda one_key: jax.random.permutation(one_key, OWNERS - 1))(row_keys)[:, :TARGETS_DEV - 1]
    owner_rows = jnp.concatenate([jnp.full((OWNERS, 1), hot_owner, jnp.int32), ((hot_owner + 1 + others) % OWNERS).astype(jnp.int32)], axis=1)
    local_rows = jax.random.randint(jax.random.fold_in(key, 14), (OWNERS, TARGETS_DEV), 0, SNB_DEV)
    targets = block_of_slot[owner_rows * SNB_DEV + local_rows]
    counts = jax.random.randint(jax.random.fold_in(key, 15), (OWNERS,), TARGETS_DEV * 3 // 4, TARGETS_DEV + 1)
    full_region = jax.random.randint(jax.random.fold_in(key, 16), (), 0, OWNERS)
    counts = counts.at[full_region].set(TARGETS_DEV)
    return (slot_of_block, targets.reshape(-1).astype(jnp.int32), counts.astype(jnp.int32))


def draw_block_slot(key, part):
    return graph_tables(key)[0]


def draw_target_block(key, part):
    return graph_tables(key)[1]


def draw_target_count(key, part):
    return graph_tables(key)[2]


def draw_latent_queries(key, part):
    base = jax.random.truncated_normal(key, -4.0, 4.0, (LATENTS, D), jnp.float32)
    return base.astype(jnp.bfloat16)


def with_ends(drawn, stream_key, low, top_value):
    longest = drawn.shape.index(max(drawn.shape))
    spots = []
    for shift in (0, 1):
        where = [jax.random.randint(jax.random.fold_in(stream_key, axis), (), 0, length) for axis, length in enumerate(drawn.shape)]
        where[longest] = (where[longest] + shift) % drawn.shape[longest]
        spots.append(tuple(where))
    return drawn.at[spots[0]].set(low).at[spots[1]].set(top_value)


def shard_levels(stream_key, dims, cuts, smallest, top_value):
    def one(axis_at, shards_of):
        steps = jax.random.uniform(jax.random.fold_in(jax.random.fold_in(stream_key, 6), axis_at), (shards_of,), jnp.float32, smallest / len(cuts), top_value / len(cuts))
        return jnp.repeat(jnp.exp(steps), dims[axis_at] // shards_of).reshape((-1,) + (1,) * (len(dims) - axis_at - 1))

    gain = one(*cuts[0])
    for cut in cuts[1:]:
        gain = gain * one(*cut)
    return gain


def noise(stream_key, shape, spread, limit, cuts=(), kind=jnp.bfloat16):
    values = jax.random.normal(stream_key, shape, jnp.float32) * spread
    if len(cuts) > 0:
        values = shard_levels(stream_key, shape, cuts, -0.22, 0.18) * values
    return jnp.clip(values, min=-limit, max=limit).astype(kind)


def setup_inputs(seed: int = 0, part: int = 0) -> dict:
    seeds = jax.random.split(jax.random.key(seed), 16)
    part_splits = jax.random.split(jax.random.fold_in(seeds[15], part), 16)
    point_features = noise(part_splits[0], (POINTS, D), 1.0, 6.0, ((0, 16),))
    point_positions = jnp.clip(1.0 * jax.random.uniform(part_splits[1], (3, POINTS), jnp.float32) ** shard_levels(part_splits[1], (3, POINTS), ((1, 16),), -0.2, 0.2), 0.0, 1.0)
    sn_positions = jnp.clip(1.0 * jax.random.uniform(part_splits[2], (3, SUPERNODES), jnp.float32) ** shard_levels(part_splits[2], (3, SUPERNODES), ((1, 16),), -0.2, 0.2), 0.0, 1.0)
    latent_queries = draw_latent_queries(jax.random.fold_in(seeds[15], 71), part)
    target_block = draw_target_block(jax.random.fold_in(jax.random.fold_in(seeds[15], part), 71), part)
    target_links = with_ends(jax.random.randint(part_splits[5], (OWNERS * TARGETS_DEV, LINKS), 0, PB_DEV), jax.random.fold_in(part_splits[5], 1), 0, PB_DEV - 1).astype(jnp.int32)
    target_count = draw_target_count(jax.random.fold_in(jax.random.fold_in(seeds[15], part), 71), part)
    block_slot = draw_block_slot(jax.random.fold_in(jax.random.fold_in(seeds[15], part), 71), part)
    w_in = noise(seeds[8], (D, D), D ** -0.5, 0.4375)
    w_mid = noise(seeds[9], (D, D), D ** -0.5, 0.4375)
    w_post = noise(seeds[10], (D, D), (D // 8) ** -0.5, 1.25)
    w_key = noise(seeds[11], (D, D), D ** -0.5, 0.4375)
    w_value = noise(seeds[12], (D, D), D ** -0.5, 0.4375)
    w_out = noise(seeds[13], (D, D), D ** -0.5, 0.4375)
    out_gain = jnp.clip(1.0 + 0.18 * jax.random.normal(seeds[14], (D,), jnp.float32), 0.1, 1.9)
    return {"point_features": point_features, "point_positions": point_positions, "sn_positions": sn_positions, "latent_queries": latent_queries, "target_block": target_block, "target_links": target_links, "target_count": target_count, "block_slot": block_slot, "w_in": w_in, "w_mid": w_mid, "w_post": w_post, "w_key": w_key, "w_value": w_value, "w_out": w_out, "out_gain": out_gain}


INV_RADIUS_SQ = 100.0

def combine_parts(first, second):
    peak_a, total_a, output_a = first
    peak_b, total_b, output_b = second
    peak = jnp.maximum(peak_a, peak_b)
    scale_a = jnp.exp(peak_a - peak)
    scale_b = jnp.exp(peak_b - peak)
    total = total_a * scale_a + total_b * scale_b
    rows = output_a.shape[0]
    heads = peak.shape[-1]
    output = output_a.reshape(rows, heads, -1) * scale_a[..., None] + output_b.reshape(rows, heads, -1) * scale_b[..., None]
    return (peak, total, output.reshape(rows, -1))

def block_attend(queries, keys_blk, values_blk):
    rows, width = queries.shape
    head_width = width // HEADS
    query_heads = queries.astype(jnp.float32).reshape(rows, HEADS, head_width)
    key_heads = keys_blk.astype(jnp.float32).reshape(-1, HEADS, head_width)
    value_heads = values_blk.astype(jnp.float32).reshape(-1, HEADS, head_width)
    scores = jnp.einsum('lhd,khd->lhk', query_heads, key_heads) * head_width ** (-0.5)
    peak = lax.optimization_barrier(jnp.max(scores, axis=-1))
    weights = jnp.exp(scores - peak[..., None])
    total = lax.optimization_barrier(jnp.sum(weights, axis=-1))
    rounded = lax.optimization_barrier(weights.astype(jnp.bfloat16)).astype(jnp.float32)
    output = jnp.einsum('lhk,khd->lhd', rounded, value_heads).reshape(rows, width)
    return (peak, total, output)

def reference(point_features, point_positions, sn_positions, latent_queries, target_block, target_links, target_count, block_slot, w_in, w_mid, w_post, w_key, w_value, w_out, out_gain):
    owners = N_PTS * N_SN
    width = point_features.shape[1]
    slot_table = block_slot[target_block].reshape(owners, TARGETS_DEV)
    live_table = jnp.arange(TARGETS_DEV)[None, :] < target_count[:, None]
    sn_blocks_all = sn_positions.reshape(3, SN_BLOCKS, BLOCK)
    region_feats = point_features.reshape(owners, PB_DEV * BLOCK, width)
    region_pos = jnp.transpose(point_positions.reshape(3, owners, PB_DEV, BLOCK), (1, 0, 2, 3))
    region_links = target_links.reshape(owners, TARGETS_DEV, LINKS)

    def per_region(carry, region):
        gathered, weight_sum = carry
        feats, positions, link_rows, slot_row, live_row = region
        inner_act = jax.nn.gelu(jnp.dot(feats, w_in, preferred_element_type=jnp.float32)).astype(jnp.bfloat16)
        hidden = jnp.dot(inner_act, w_mid, preferred_element_type=jnp.float32).astype(jnp.bfloat16)
        hidden_blocks = hidden.reshape(PB_DEV, BLOCK, width)
        target_pos = sn_blocks_all[:, slot_row]
        linked_pos = positions[:, link_rows]
        gaps = target_pos[:, :, None, :, None] - linked_pos[:, :, :, None, :]
        kernel = 1.0 / (1.0 + lax.optimization_barrier(jnp.sum(gaps * gaps, axis=0)) * INV_RADIUS_SQ)
        totals = lax.optimization_barrier(jnp.sum(kernel, axis=(1, 3)))
        rounded = lax.optimization_barrier(kernel.astype(jnp.bfloat16)).astype(jnp.float32)
        sums = jnp.einsum('tlji,tlic->tjc', rounded, hidden_blocks[link_rows].astype(jnp.float32))
        sums = jnp.where(live_row[:, None, None], sums, 0.0).astype(jnp.bfloat16)
        totals = jnp.where(live_row[:, None], totals, 0.0).astype(jnp.bfloat16)
        sums = lax.optimization_barrier(sums).astype(jnp.float32)
        totals = lax.optimization_barrier(totals).astype(jnp.float32)
        gathered = gathered.at[slot_row].add(sums)
        weight_sum = weight_sum.at[slot_row].add(totals)
        return ((gathered, weight_sum), None)
    start = (jnp.zeros((SN_BLOCKS, BLOCK, width), jnp.float32), jnp.zeros((SN_BLOCKS, BLOCK), jnp.float32))
    (gathered, weight_sum), unused = lax.scan(per_region, start, (region_feats, region_pos, region_links, slot_table, live_table))
    pooled = (gathered / (1.0 + weight_sum[..., None])).astype(jnp.bfloat16).reshape(SUPERNODES, width)
    supernode_features = jax.nn.gelu(jnp.dot(pooled, w_post, preferred_element_type=jnp.float32)).astype(jnp.bfloat16)
    keys = jnp.dot(supernode_features, w_key, preferred_element_type=jnp.float32).astype(jnp.bfloat16)
    values = jnp.dot(supernode_features, w_value, preferred_element_type=jnp.float32).astype(jnp.bfloat16)
    rows = latent_queries.shape[0]
    init = (jnp.full((rows, HEADS), -jnp.inf, jnp.float32), jnp.zeros((rows, HEADS), jnp.float32), jnp.zeros((rows, width), jnp.float32))

    def key_step(carry, block_inputs):
        return (combine_parts(carry, block_attend(latent_queries, block_inputs[0], block_inputs[1])), None)
    partial_state, unused = lax.scan(key_step, init, (keys.reshape(-1, KEY_BLOCK, width), values.reshape(-1, KEY_BLOCK, width)))
    peak, total, output = partial_state
    attended = (output.reshape(rows, HEADS, -1) / total[..., None]).reshape(rows, width).astype(jnp.bfloat16)
    projected = jnp.dot(attended, w_out, preferred_element_type=jnp.float32)
    mean_sq = lax.optimization_barrier(jnp.mean(projected * projected, axis=-1, keepdims=True))
    latent_out = (projected * lax.rsqrt(mean_sq + 1e-06) * out_gain.astype(jnp.float32)).astype(jnp.bfloat16)
    return (supernode_features, latent_out)
```

```python
import functools

import jax
import jax.numpy as jnp
from jax import lax
from jax.experimental import pallas as pl
from jax.experimental.pallas import tpu as pltpu
from jax.sharding import PartitionSpec as P

HEADS = 3
BLOCK = 128
INV_RADIUS_SQ = 100.0
MESH = pl.DeviceIdType.MESH
STAT_ROWS = 16
CHUNK = 512
LATENT_CHUNK = 256
OUT_LANES = 256
F32 = jnp.float32
BF16 = jnp.bfloat16


def contract(a, b, dim_a, dim_b):
    return lax.dot_general(a, b, (((dim_a,), (dim_b,)), ((), ())), preferred_element_type=F32)


def place(n_sn):
    return lax.axis_index("pts") * n_sn + lax.axis_index("sn")


def peer(index, n_sn):
    return {"pts": lax.div(index, n_sn), "sn": lax.rem(index, n_sn)}


def greet(owners, me, n_sn):
    barrier = pltpu.get_barrier_semaphore()

    def signal(off, carry):
        other = lax.rem(me + off, owners)
        pl.semaphore_signal(barrier, inc=1, device_id=peer(other, n_sn), device_id_type=MESH)
        return carry

    lax.fori_loop(1, owners, signal, 0)
    pl.semaphore_wait(barrier, owners - 1)


def columns_of(rows):
    padded = jnp.concatenate([rows, jnp.zeros((5, rows.shape[1]), F32)], axis=0)
    return jnp.transpose(padded)


def message_kernel(
    owners,
    n_sn,
    sn_blocks,
    targets,
    target_block,
    target_links,
    target_count,
    block_slot,
    feats,
    positions,
    sn_positions,
    w_in,
    w_mid,
    arrived,
    everywhere,
    hidden,
    point_blocks,
    outgoing,
    slots,
    pos_send,
    pos_recv,
    msg_send,
    msg_recv,
    own_sem,
):
    me = place(n_sn)
    links = target_links.shape[1]
    width = feats.shape[1]
    greet(owners, me, n_sn)

    def pos_copy(other, slot_at):
        return pltpu.make_async_remote_copy(
            src_ref=sn_positions,
            dst_ref=everywhere.at[slot_at],
            send_sem=pos_send.at[other],
            recv_sem=pos_recv.at[slot_at],
            device_id=peer(other, n_sn),
            device_id_type=MESH,
        )

    def start_pos(off, carry):
        pos_copy(lax.rem(me + off, owners), me).start()
        return carry

    lax.fori_loop(1, owners, start_pos, 0)
    own_pos = pltpu.make_async_copy(sn_positions, everywhere.at[me], own_sem.at[0])
    own_pos.start()

    def slot_of(k, carry):
        slots[k] = block_slot[target_block[me * targets + k]]
        return carry

    lax.fori_loop(0, targets, slot_of, 0)
    my_count = target_count[me]

    def mlp(step, carry):
        rows = feats[pl.ds(pl.multiple_of(step * CHUNK, CHUNK), CHUNK), :]
        inner = jax.nn.gelu(contract(w_in[...], rows, 0, 1)).astype(BF16)
        hid = contract(w_mid[...], inner, 0, 0).astype(BF16)
        places = positions[:, pl.ds(pl.multiple_of(step * CHUNK, CHUNK), CHUNK)]
        for q in range(CHUNK // BLOCK):
            hidden[step * (CHUNK // BLOCK) + q] = hid[:, q * BLOCK : (q + 1) * BLOCK]
            point_blocks[step * (CHUNK // BLOCK) + q] = places[:, q * BLOCK : (q + 1) * BLOCK]
        return carry

    lax.fori_loop(0, feats.shape[0] // CHUNK, mlp, 0)

    def wait_pos(off, carry):
        other = lax.rem(me + off, owners)
        copy = pos_copy(other, other)
        copy.wait_send()
        copy.wait_recv()
        return carry

    own_pos.wait()
    lax.fori_loop(1, owners, wait_pos, 0)

    def msg_copy(other, slot_at):
        return pltpu.make_async_remote_copy(
            src_ref=outgoing.at[other],
            dst_ref=arrived.at[slot_at],
            send_sem=msg_send.at[other],
            recv_sem=msg_recv.at[slot_at],
            device_id=peer(other, n_sn),
            device_id_type=MESH,
        )

    def build(other):
        def look(k, state):
            which, block, live = state
            slot = slots[k]
            hit = jnp.logical_and(lax.div(slot, sn_blocks) == other, k < my_count)
            return (
                jnp.where(hit, k, which),
                jnp.where(hit, lax.rem(slot, sn_blocks), block),
                jnp.where(hit, 1.0, live),
            )

        start = (jnp.int32(0), jnp.int32(0), F32(0.0))
        which, block, live = lax.fori_loop(0, targets, look, start, unroll=targets <= 8)
        candidates = everywhere[other]
        sn_rows = candidates[:, :BLOCK]
        for b in range(1, sn_blocks):
            sn_rows = jnp.where(block == b, candidates[:, b * BLOCK : (b + 1) * BLOCK], sn_rows)
        sn_cols = columns_of(sn_rows)
        kernels = []
        blocks = []
        for j in range(links):
            link = target_links[which, j]
            pts = point_blocks[link]
            dist = jnp.zeros((BLOCK, BLOCK), F32)
            for c in range(3):
                gap = sn_cols[:, c : c + 1] - pts[c : c + 1, :]
                dist = dist + gap * gap
            kernels.append(1.0 / (1.0 + dist * INV_RADIUS_SQ))
            blocks.append(hidden[link])
        total = kernels[0]
        for extra in kernels[1:]:
            total = total + extra
        total = jnp.sum(jnp.transpose(total), axis=0, keepdims=True)
        message = contract(
            jnp.concatenate(blocks, axis=1),
            jnp.concatenate([one.astype(BF16) for one in kernels], axis=1),
            1,
            1,
        )
        outgoing[other, :width, :] = (message * live).astype(BF16)
        outgoing[other, width:, :] = jnp.broadcast_to(total * live, (STAT_ROWS, BLOCK)).astype(BF16)

    def send(off, carry):
        other = lax.rem(me + off, owners)
        build(other)
        msg_copy(other, me).start()
        return carry

    lax.fori_loop(1, owners, send, 0)
    build(me)
    own = pltpu.make_async_copy(outgoing.at[me], arrived.at[me], own_sem.at[1])
    own.start()
    own.wait()

    def finish(off, carry):
        other = lax.rem(me + off, owners)
        copy = msg_copy(other, other)
        copy.wait_send()
        copy.wait_recv()
        return carry

    lax.fori_loop(1, owners, finish, 0)


def thirds(x):
    first = x.astype(BF16).astype(F32)
    second = (x - first).astype(BF16).astype(F32)
    third = x - first - second
    return [first, second, third]


def attend_kernel(
    owners,
    n_sn,
    sn_blocks,
    targets,
    target_block,
    block_slot,
    arrived,
    queries,
    w_post,
    w_key,
    w_value,
    features_out,
    partial_out,
    sums,
    pooled,
):
    me = place(n_sn)
    width = queries.shape[1]
    head_width = width // HEADS
    rows = queries.shape[0]
    sums[...] = jnp.zeros_like(sums)

    def add(source, carry):
        def look(k, block):
            slot = block_slot[target_block[source * targets + k]]
            return jnp.where(lax.div(slot, sn_blocks) == me, lax.rem(slot, sn_blocks), block)

        block = lax.fori_loop(0, targets, look, jnp.int32(0), unroll=targets <= 8)
        sums[block] += arrived[source].astype(F32)
        return carry

    lax.fori_loop(0, owners, add, 0)
    for b in range(sn_blocks):
        scale = 1.0 / (1.0 + sums[b, width : width + 1, :])
        pooled[:, b * BLOCK : (b + 1) * BLOCK] = (sums[b, :width, :] * scale).astype(BF16)
    features = jax.nn.gelu(contract(pooled[...], w_post[...], 0, 0)).astype(BF16)
    features_out[...] = features
    keys = contract(features, w_key[...], 1, 0).astype(BF16)
    values_t = contract(w_value[...], features, 0, 1).astype(BF16)
    head_of = lax.broadcasted_iota(jnp.int32, (LATENT_CHUNK, width), 1) // head_width
    for at in range(0, rows, LATENT_CHUNK):
        part = queries[at : at + LATENT_CHUNK, :] * BF16(head_width ** (-0.5))
        outs, peaks, totals = [], [], []
        for h in range(HEADS):
            scores = contract(keys, jnp.where(head_of == h, part, BF16(0.0)), 1, 1)
            peak = jnp.max(scores, axis=0, keepdims=True)
            probs = jnp.exp(scores - peak)
            totals += thirds(jnp.sum(probs, axis=0, keepdims=True))
            peaks += thirds(peak)
            outs.append(
                contract(
                    values_t[h * head_width : (h + 1) * head_width, :], probs.astype(BF16), 1, 0
                )
            )
        pad = jnp.zeros((OUT_LANES - width - 6 * HEADS, LATENT_CHUNK), F32)
        whole = jnp.concatenate(outs + peaks + totals + [pad], axis=0)
        partial_out[at : at + LATENT_CHUNK, :] = jnp.transpose(whole).astype(BF16)


def merge_kernel(
    owners, n_sn, parts, w_out, out_gain, latent_out, arrived, send_sem, recv_sem, own_sem
):
    me = place(n_sn)
    width = w_out.shape[0]
    head_width = width // HEADS
    share = parts.shape[1]
    greet(owners, me, n_sn)

    def copy_of(other, slot_at):
        return pltpu.make_async_remote_copy(
            src_ref=parts.at[other],
            dst_ref=arrived.at[slot_at],
            send_sem=send_sem.at[other],
            recv_sem=recv_sem.at[slot_at],
            device_id=peer(other, n_sn),
            device_id_type=MESH,
        )

    def start(off, carry):
        copy_of(lax.rem(me + off, owners), me).start()
        return carry

    lax.fori_loop(1, owners, start, 0)
    own = pltpu.make_async_copy(parts.at[me], arrived.at[me], own_sem)
    own.start()
    own.wait()

    def finish(off, carry):
        other = lax.rem(me + off, owners)
        copy = copy_of(other, other)
        copy.wait_send()
        copy.wait_recv()
        return carry

    lax.fori_loop(1, owners, finish, 0)
    head_of = lax.broadcasted_iota(jnp.int32, (share, width), 1) // head_width

    def spread(columns):
        full = jnp.broadcast_to(columns[HEADS - 1], (share, width))
        for h in range(HEADS - 2, -1, -1):
            full = jnp.where(head_of == h, columns[h], full)
        return full

    def stat(block, at):
        return spread(
            [
                block[:, at + 3 * h : at + 3 * h + 1]
                + block[:, at + 3 * h + 1 : at + 3 * h + 2]
                + block[:, at + 3 * h + 2 : at + 3 * h + 3]
                for h in range(HEADS)
            ]
        )

    def load(source):
        block = arrived[source].astype(F32)
        return block[:, :width], stat(block, width), stat(block, width + 3 * HEADS)

    def combine(source, state):
        output, peak, total = state
        new_output, new_peak, new_total = load(source)
        top = jnp.maximum(peak, new_peak)
        scale, new_scale = jnp.exp(peak - top), jnp.exp(new_peak - top)
        return (
            output * scale + new_output * new_scale,
            top,
            total * scale + new_total * new_scale,
        )

    output, peak, total = lax.fori_loop(1, owners, combine, load(0), unroll=owners <= 16)
    attended = (output / total).astype(BF16)
    projected = jnp.dot(attended, w_out[...], preferred_element_type=F32)
    mean_sq = jnp.mean(projected * projected, axis=-1, keepdims=True)
    latent_out[...] = (projected * lax.rsqrt(mean_sq + 1e-06) * out_gain[...]).astype(BF16)


def per_device(
    n_sn,
    owners,
    point_features,
    point_positions,
    sn_positions,
    latent_queries,
    target_block,
    target_links,
    target_count,
    block_slot,
    w_in,
    w_mid,
    w_post,
    w_key,
    w_value,
    w_out,
    out_gain,
):
    targets = target_links.shape[0]
    width = point_features.shape[1]
    sn_rows = sn_positions.shape[1]
    sn_blocks = sn_rows // BLOCK
    latents = latent_queries.shape[0]
    share = latents // owners
    smem = pl.BlockSpec(memory_space=pltpu.SMEM)
    vmem = pl.BlockSpec(memory_space=pltpu.VMEM)
    dma = pltpu.SemaphoreType.DMA
    arrived = pl.pallas_call(
        functools.partial(message_kernel, owners, n_sn, sn_blocks, targets),
        out_shape=jax.ShapeDtypeStruct((owners, width + STAT_ROWS, BLOCK), BF16),
        in_specs=[smem] * 4 + [vmem] * 5,
        out_specs=pl.BlockSpec(memory_space=pl.ANY),
        scratch_shapes=[
            pltpu.VMEM((owners, 3, sn_rows), F32),
            pltpu.VMEM((point_features.shape[0] // BLOCK, width, BLOCK), BF16),
            pltpu.VMEM((point_features.shape[0] // BLOCK, 3, BLOCK), F32),
            pltpu.VMEM((owners, width + STAT_ROWS, BLOCK), BF16),
            pltpu.SMEM((targets,), jnp.int32),
            dma((owners,)),
            dma((owners,)),
            dma((owners,)),
            dma((owners,)),
            dma((2,)),
        ],
        compiler_params=pltpu.CompilerParams(collective_id=0, has_side_effects=True),
        name="messages",
    )(
        target_block,
        target_links,
        target_count,
        block_slot,
        point_features,
        point_positions,
        sn_positions,
        w_in,
        w_mid,
    )
    features, partial = pl.pallas_call(
        functools.partial(attend_kernel, owners, n_sn, sn_blocks, targets),
        out_shape=(
            jax.ShapeDtypeStruct((sn_rows, width), BF16),
            jax.ShapeDtypeStruct((latents, OUT_LANES), BF16),
        ),
        in_specs=[smem] * 2 + [vmem] * 5,
        out_specs=(vmem, vmem),
        scratch_shapes=[
            pltpu.VMEM((sn_blocks, width + STAT_ROWS, BLOCK), F32),
            pltpu.VMEM((width, sn_rows), BF16),
        ],
        name="attend",
    )(target_block, block_slot, arrived, latent_queries, w_post, w_key, w_value)
    latent_out = pl.pallas_call(
        functools.partial(merge_kernel, owners, n_sn),
        out_shape=jax.ShapeDtypeStruct((share, width), BF16),
        in_specs=[vmem] * 3,
        out_specs=vmem,
        scratch_shapes=[
            pltpu.VMEM((owners, share, OUT_LANES), BF16),
            dma((owners,)),
            dma((owners,)),
            dma,
        ],
        compiler_params=pltpu.CompilerParams(collective_id=1, has_side_effects=True),
        name="merge",
    )(partial.reshape(owners, share, OUT_LANES), w_out, out_gain.reshape(1, width))
    return (features, latent_out)


def solution(mesh):
    n_sn = mesh.shape["sn"]
    owners = mesh.shape["pts"] * n_sn
    everything = ("groups", "pts", "sn")
    in_specs = (
        P(everything, None),
        P(None, everything),
        P(None, everything),
        P(),
        P("groups"),
        P(everything, None),
        P("groups"),
        P("groups"),
        P(),
        P(),
        P(),
        P(),
        P(),
        P(),
        P(),
    )
    out_specs = (P(everything, None), P(everything, None))
    return jax.shard_map(
        functools.partial(per_device, n_sn, owners),
        mesh=mesh,
        in_specs=in_specs,
        out_specs=out_specs,
        check_vma=False,
    )
```

```python
import functools

import jax
import jax.numpy as jnp
from jax import lax
from jax.experimental import pallas as pl
from jax.experimental.pallas import tpu as pltpu
from jax.sharding import PartitionSpec as P

HEADS = 3
BLOCK = 128
INV_RADIUS_SQ = 100.0
MESH = pl.DeviceIdType.MESH
STAT_ROWS = 8
CHUNK = 512
LATENT_CHUNK = 256
OUT_LANES = 256
F32 = jnp.float32
BF16 = jnp.bfloat16


def contract(a, b, dim_a, dim_b):
    return lax.dot_general(a, b, (((dim_a,), (dim_b,)), ((), ())), preferred_element_type=F32)


def place(n_sn):
    return lax.axis_index("pts") * n_sn + lax.axis_index("sn")


def peer(index, n_sn):
    return {"pts": lax.div(index, n_sn), "sn": lax.rem(index, n_sn)}


def greet(owners, me, n_sn):
    barrier = pltpu.get_barrier_semaphore()

    def signal(off, carry):
        other = lax.rem(me + off, owners)
        pl.semaphore_signal(barrier, inc=1, device_id=peer(other, n_sn), device_id_type=MESH)
        return carry

    lax.fori_loop(1, owners, signal, 0)
    return barrier


def far_first(i, owners):
    return owners // 2 + lax.div(i + 1, 2) * (2 * lax.rem(i + 1, 2) - 1)


def named_block(owner, targets, sn_blocks, count, slot_at):
    def look(k, state):
        which, block, live = state
        slot = slot_at(k)
        hit = jnp.logical_and(lax.div(slot, sn_blocks) == owner, k < count)
        return (
            jnp.where(hit, k, which),
            jnp.where(hit, lax.rem(slot, sn_blocks), block),
            jnp.where(hit, 1.0, live),
        )

    start = (jnp.int32(0), jnp.int32(0), F32(0.0))
    return lax.fori_loop(0, targets, look, start, unroll=targets <= 8)


def columns_of(rows):
    padded = jnp.concatenate([rows, jnp.zeros((5, rows.shape[1]), F32)], axis=0)
    return jnp.transpose(padded)


def message_kernel(
    owners,
    n_sn,
    sn_blocks,
    targets,
    target_block,
    target_links,
    target_count,
    block_slot,
    feats,
    positions,
    sn_positions,
    w_in,
    w_mid,
    arrived,
    points,
    wanted,
    everywhere,
    hidden,
    point_blocks,
    outgoing,
    slots,
    pos_send,
    pos_recv,
    msg_send,
    msg_recv,
    own_sem,
):
    me = place(n_sn)
    links = target_links.shape[0]
    width = feats.shape[0]
    barrier = greet(owners, me, n_sn)
    load = pltpu.make_async_copy(feats, points, own_sem.at[2])
    load.start()

    def choose(region, carry):
        def slot_at(k):
            return block_slot[target_block[region * targets + k]]

        block = named_block(me, targets, sn_blocks, target_count[region], slot_at)[1]
        rows = sn_positions[:, :BLOCK]
        for b in range(1, sn_blocks):
            rows = jnp.where(block == b, sn_positions[:, b * BLOCK : (b + 1) * BLOCK], rows)
        wanted[region] = rows
        return carry

    lax.fori_loop(0, owners, choose, 0)

    def slot_of(k, carry):
        slots[k] = block_slot[target_block[me * targets + k]]
        return carry

    lax.fori_loop(0, targets, slot_of, 0)
    my_count = target_count[me]

    def pos_copy(other, slot_at):
        return pltpu.make_async_remote_copy(
            src_ref=wanted.at[other],
            dst_ref=everywhere.at[slot_at],
            send_sem=pos_send.at[other],
            recv_sem=pos_recv.at[slot_at],
            device_id=peer(other, n_sn),
            device_id_type=MESH,
        )

    def start_pos(i, carry):
        pos_copy(lax.rem(me + far_first(i, owners), owners), me).start()
        return carry

    pl.semaphore_wait(barrier, owners - 1)
    lax.fori_loop(0, owners - 1, start_pos, 0)
    own_pos = pltpu.make_async_copy(wanted.at[me], everywhere.at[me], own_sem.at[0])
    own_pos.start()
    load.wait()

    def mlp(step, carry):
        span = pl.ds(pl.multiple_of(step * CHUNK, CHUNK), CHUNK)
        inner = jax.nn.gelu(contract(w_in[...], points[:, span], 0, 0)).astype(BF16)
        hid = contract(w_mid[...], inner, 0, 0).astype(BF16)
        places = positions[:, span]
        for q in range(CHUNK // BLOCK):
            hidden[step * (CHUNK // BLOCK) + q] = hid[:, q * BLOCK : (q + 1) * BLOCK]
            point_blocks[step * (CHUNK // BLOCK) + q] = places[:, q * BLOCK : (q + 1) * BLOCK]
        return carry

    lax.fori_loop(0, feats.shape[1] // CHUNK, mlp, 0)

    def wait_pos(off, carry):
        other = lax.rem(me + off, owners)
        copy = pos_copy(other, other)
        copy.wait_send()
        copy.wait_recv()
        return carry

    own_pos.wait()
    lax.fori_loop(1, owners, wait_pos, 0)

    def msg_copy(other, slot_at):
        return pltpu.make_async_remote_copy(
            src_ref=outgoing.at[other],
            dst_ref=arrived.at[slot_at],
            send_sem=msg_send.at[other],
            recv_sem=msg_recv.at[slot_at],
            device_id=peer(other, n_sn),
            device_id_type=MESH,
        )

    def build(other):
        which, block, live = named_block(
            other, targets, sn_blocks, my_count, lambda k: slots[k]
        )
        sn_cols = columns_of(everywhere[other])
        kernels = []
        blocks = []
        for j in range(links):
            link = target_links[j, which]
            pts = point_blocks[link]
            dist = jnp.zeros((BLOCK, BLOCK), F32)
            for c in range(3):
                gap = sn_cols[:, c : c + 1] - pts[c : c + 1, :]
                dist = dist + gap * gap
            kernels.append(1.0 / (1.0 + dist * INV_RADIUS_SQ))
            blocks.append(hidden[link])
        total = kernels[0]
        for extra in kernels[1:]:
            total = total + extra
        total = jnp.sum(jnp.transpose(total), axis=0, keepdims=True)
        message = contract(
            jnp.concatenate(blocks, axis=1),
            jnp.concatenate([one.astype(BF16) for one in kernels], axis=1),
            1,
            1,
        )
        outgoing[other, :width, :] = (message * live).astype(BF16)
        outgoing[other, width:, :] = jnp.broadcast_to(total * live, (STAT_ROWS, BLOCK)).astype(BF16)

    def nth(i):
        return lax.rem(me + far_first(i, owners), owners)

    build(nth(0))

    def send(i, carry):
        build(nth(i))
        msg_copy(nth(i - 1), me).start()
        return carry

    lax.fori_loop(1, owners - 1, send, 0)
    build(me)
    msg_copy(nth(owners - 2), me).start()
    own = pltpu.make_async_copy(outgoing.at[me], arrived.at[me], own_sem.at[1])
    own.start()
    own.wait()

    def finish(off, carry):
        other = lax.rem(me + off, owners)
        copy = msg_copy(other, other)
        copy.wait_send()
        copy.wait_recv()
        return carry

    lax.fori_loop(1, owners, finish, 0)


def thirds(x):
    first = x.astype(BF16).astype(F32)
    second = (x - first).astype(BF16).astype(F32)
    third = x - first - second
    return [first, second, third]


def pool_kernel(
    owners, n_sn, sn_blocks, targets, target_block, block_slot, arrived, w_post, features_out, sums, pooled
):
    me = place(n_sn)
    width = w_post.shape[0]
    sums[...] = jnp.zeros_like(sums)

    def add(source, carry):
        def look(k, block):
            slot = block_slot[target_block[source * targets + k]]
            return jnp.where(lax.div(slot, sn_blocks) == me, lax.rem(slot, sn_blocks), block)

        block = lax.fori_loop(0, targets, look, jnp.int32(0), unroll=targets <= 8)
        sums[block] += arrived[source].astype(F32)
        return carry

    lax.fori_loop(0, owners, add, 0)
    for b in range(sn_blocks):
        scale = 1.0 / (1.0 + sums[b, width : width + 1, :])
        pooled[:, b * BLOCK : (b + 1) * BLOCK] = (sums[b, :width, :] * scale).astype(BF16)
    features_out[...] = jax.nn.gelu(contract(w_post[...], pooled[...], 0, 0)).astype(BF16)


def attend_kernel(
    owners,
    n_sn,
    features,
    queries,
    w_key,
    w_value,
    w_out,
    out_gain,
    latent_out,
    values_t,
    keys,
    parts,
    arrived,
    send_sem,
    recv_sem,
    own_sem,
):
    me = place(n_sn)
    width, latents = queries.shape
    head_width = width // HEADS
    share = latents // owners
    chunks = latents // LATENT_CHUNK
    per_chunk = LATENT_CHUNK // share
    barrier = greet(owners, me, n_sn)
    keys[...] = contract(features[...], w_key[...], 0, 0).astype(BF16)
    values_t[...] = contract(w_value[...], features[...], 0, 0).astype(BF16)
    row_head = lax.broadcasted_iota(jnp.int32, (width, LATENT_CHUNK), 0) // head_width
    first = lax.div(me, per_chunk) + chunks // 2

    def attend(step, carry):
        chunk = lax.rem(first + step, chunks)
        at = pl.multiple_of(chunk * LATENT_CHUNK, LATENT_CHUNK)
        part = queries[:, pl.ds(at, LATENT_CHUNK)] * BF16(head_width ** (-0.5))
        outs, peaks, totals = [], [], []
        for h in range(HEADS):
            scores = contract(keys[...], jnp.where(row_head == h, part, BF16(0.0)), 1, 0)
            peak = jnp.max(scores, axis=0, keepdims=True)
            probs = jnp.exp(scores - peak)
            totals += thirds(jnp.sum(probs, axis=0, keepdims=True))
            peaks += thirds(peak)
            own_values = values_t[h * head_width : (h + 1) * head_width, :]
            outs.append(contract(own_values, probs.astype(BF16), 1, 0))
        pad = jnp.zeros((OUT_LANES - width - 6 * HEADS, LATENT_CHUNK), F32)
        whole = jnp.transpose(jnp.concatenate(outs + peaks + totals + [pad], axis=0))
        for j in range(per_chunk):
            parts[chunk * per_chunk + j] = whole[j * share : (j + 1) * share, :].astype(BF16)
        return carry

    def copy_of(other, slot_at):
        return pltpu.make_async_remote_copy(
            src_ref=parts.at[other],
            dst_ref=arrived.at[slot_at],
            send_sem=send_sem.at[other],
            recv_sem=recv_sem.at[slot_at],
            device_id=peer(other, n_sn),
            device_id_type=MESH,
        )

    def send_chunk(step):
        chunk = lax.rem(first + step, chunks)

        def start(j, carry):
            other = chunk * per_chunk + lax.rem(me + j, per_chunk)

            @pl.when(other != me)
            def _():
                copy_of(other, me).start()

            return carry

        lax.fori_loop(0, per_chunk, start, 0)

    attend(0, 0)
    pl.semaphore_wait(barrier, owners - 1)

    def step_on(step, carry):
        send_chunk(step - 1)
        return attend(step, carry)

    lax.fori_loop(1, chunks, step_on, 0)
    send_chunk(chunks - 1)
    own = pltpu.make_async_copy(parts.at[me], arrived.at[me], own_sem)
    own.start()
    own.wait()

    def finish(off, carry):
        other = lax.rem(me + off, owners)
        copy = copy_of(other, other)
        copy.wait_send()
        copy.wait_recv()
        return carry

    lax.fori_loop(1, owners, finish, 0)
    lane = lax.broadcasted_iota(jnp.int32, (OUT_LANES, width), 0) - width
    head_of = lax.broadcasted_iota(jnp.int32, (OUT_LANES, width), 1) // head_width
    is_peak = jnp.logical_and(lane >= 3 * head_of, lane < 3 * head_of + 3)
    total_lane = lane - 3 * HEADS
    is_total = jnp.logical_and(total_lane >= 3 * head_of, total_lane < 3 * head_of + 3)
    flat = jnp.concatenate([arrived[source] for source in range(owners)], axis=0)
    peaks = contract(flat, jnp.where(is_peak, 1.0, 0.0).astype(BF16), 1, 0)
    totals = contract(flat, jnp.where(is_total, 1.0, 0.0).astype(BF16), 1, 0)

    def of(full, source):
        return full[source * share : (source + 1) * share, :]

    top = of(peaks, 0)
    for source in range(1, owners):
        top = jnp.maximum(top, of(peaks, source))
    output = jnp.zeros((share, width), F32)
    total = jnp.zeros((share, width), F32)
    for source in range(owners):
        scale = jnp.exp(of(peaks, source) - top)
        output = output + scale * arrived[source][:, :width].astype(F32)
        total = total + scale * of(totals, source)
    attended = (output / total).astype(BF16)
    projected = jnp.dot(attended, w_out[...], preferred_element_type=F32)
    mean_sq = jnp.mean(projected * projected, axis=-1, keepdims=True)
    latent_out[...] = (projected * lax.rsqrt(mean_sq + 1e-06) * out_gain[...]).astype(BF16)


def per_device(
    n_sn,
    owners,
    point_features,
    point_positions,
    sn_positions,
    latent_queries,
    target_block,
    target_links,
    target_count,
    block_slot,
    w_in,
    w_mid,
    w_post,
    w_key,
    w_value,
    w_out,
    out_gain,
):
    targets = target_links.shape[0]
    width = point_features.shape[1]
    sn_rows = sn_positions.shape[1]
    sn_blocks = sn_rows // BLOCK
    latents = latent_queries.shape[0]
    share = latents // owners
    smem = pl.BlockSpec(memory_space=pltpu.SMEM)
    vmem = pl.BlockSpec(memory_space=pltpu.VMEM)
    hbm = pl.BlockSpec(memory_space=pl.ANY)
    dma = pltpu.SemaphoreType.DMA
    arrived = pl.pallas_call(
        functools.partial(message_kernel, owners, n_sn, sn_blocks, targets),
        out_shape=jax.ShapeDtypeStruct((owners, width + STAT_ROWS, BLOCK), BF16),
        in_specs=[smem] * 4 + [hbm] + [vmem] * 4,
        out_specs=pl.BlockSpec(memory_space=pl.ANY),
        scratch_shapes=[
            pltpu.VMEM(point_features.shape[::-1], BF16),
            pltpu.VMEM((owners, 3, BLOCK), F32),
            pltpu.VMEM((owners, 3, BLOCK), F32),
            pltpu.VMEM((point_features.shape[0] // BLOCK, width, BLOCK), BF16),
            pltpu.VMEM((point_features.shape[0] // BLOCK, 3, BLOCK), F32),
            pltpu.VMEM((owners, width + STAT_ROWS, BLOCK), BF16),
            pltpu.SMEM((targets,), jnp.int32),
            dma((owners,)),
            dma((owners,)),
            dma((owners,)),
            dma((owners,)),
            dma((3,)),
        ],
        compiler_params=pltpu.CompilerParams(collective_id=0, has_side_effects=True),
        name="messages",
    )(
        target_block,
        target_links.T,
        target_count,
        block_slot,
        point_features.T,
        point_positions,
        sn_positions,
        w_in,
        w_mid,
    )
    features_t = pl.pallas_call(
        functools.partial(pool_kernel, owners, n_sn, sn_blocks, targets),
        out_shape=jax.ShapeDtypeStruct((width, sn_rows), BF16),
        in_specs=[smem] * 2 + [vmem] * 2,
        out_specs=vmem,
        scratch_shapes=[
            pltpu.VMEM((sn_blocks, width + STAT_ROWS, BLOCK), F32),
            pltpu.VMEM((width, sn_rows), BF16),
        ],
        name="pool",
    )(target_block, block_slot, arrived, w_post)
    latent_out = pl.pallas_call(
        functools.partial(attend_kernel, owners, n_sn),
        out_shape=jax.ShapeDtypeStruct((share, width), BF16),
        in_specs=[vmem] * 6,
        out_specs=vmem,
        scratch_shapes=[
            pltpu.VMEM((width, sn_rows), BF16),
            pltpu.VMEM((sn_rows, width), BF16),
            pltpu.VMEM((owners, share, OUT_LANES), BF16),
            pltpu.VMEM((owners, share, OUT_LANES), BF16),
            dma((owners,)),
            dma((owners,)),
            dma,
        ],
        compiler_params=pltpu.CompilerParams(collective_id=1, has_side_effects=True),
        name="attend",
    )(features_t, latent_queries.T, w_key, w_value, w_out, out_gain.reshape(1, width))
    return (features_t.T, latent_out)


def solution(mesh):
    n_sn = mesh.shape["sn"]
    owners = mesh.shape["pts"] * n_sn
    everything = ("groups", "pts", "sn")
    in_specs = (
        P(everything, None),
        P(None, everything),
        P(None, everything),
        P(),
        P("groups"),
        P(everything, None),
        P("groups"),
        P("groups"),
        P(),
        P(),
        P(),
        P(),
        P(),
        P(),
        P(),
    )
    out_specs = (P(everything, None), P(everything, None))
    return jax.shard_map(
        functools.partial(per_device, n_sn, owners),
        mesh=mesh,
        in_specs=in_specs,
        out_specs=out_specs,
        check_vma=False,
    )
```

```python
import functools

import jax
import jax.numpy as jnp
from jax import lax
from jax.experimental import pallas as pl
from jax.experimental.pallas import tpu as pltpu
from jax.sharding import PartitionSpec as P

HEADS = 3
BLOCK = 128
INV_RADIUS_SQ = 100.0
MESH = pl.DeviceIdType.MESH
STAT_ROWS = 8
CHUNK = 512
LATENT_CHUNK = 256
OUT_LANES = 256
F32 = jnp.float32
BF16 = jnp.bfloat16


def contract(a, b, dim_a, dim_b):
    return lax.dot_general(a, b, (((dim_a,), (dim_b,)), ((), ())), preferred_element_type=F32)


def place(n_sn):
    return lax.axis_index("pts") * n_sn + lax.axis_index("sn")


def peer(index, n_sn):
    return {"pts": lax.div(index, n_sn), "sn": lax.rem(index, n_sn)}


def greet(owners, me, n_sn):
    barrier = pltpu.get_barrier_semaphore()

    def signal(off, carry):
        other = lax.rem(me + off, owners)
        pl.semaphore_signal(barrier, inc=1, device_id=peer(other, n_sn), device_id_type=MESH)
        return carry

    lax.fori_loop(1, owners, signal, 0)
    return barrier


def far_first(i, owners):
    return owners // 2 + lax.div(i + 1, 2) * (2 * lax.rem(i + 1, 2) - 1)


def named_block(owner, targets, sn_blocks, count, slot_at):
    def look(k, state):
        which, block, live = state
        slot = slot_at(k)
        hit = jnp.logical_and(lax.div(slot, sn_blocks) == owner, k < count)
        return (
            jnp.where(hit, k, which),
            jnp.where(hit, lax.rem(slot, sn_blocks), block),
            jnp.where(hit, 1.0, live),
        )

    start = (jnp.int32(0), jnp.int32(0), F32(0.0))
    return lax.fori_loop(0, targets, look, start, unroll=targets <= 8)


def columns_of(rows):
    padded = jnp.concatenate([rows, jnp.zeros((5, rows.shape[1]), F32)], axis=0)
    return jnp.transpose(padded)


def message_kernel(
    owners,
    n_sn,
    sn_blocks,
    targets,
    target_block,
    target_links,
    target_count,
    block_slot,
    feats,
    positions,
    sn_positions,
    w_in,
    w_mid,
    pooled,
    arrived,
    sums,
    block_of,
    points,
    wanted,
    everywhere,
    hidden,
    point_blocks,
    outgoing,
    slots,
    pos_send,
    pos_recv,
    msg_send,
    msg_recv,
    own_sem,
):
    me = place(n_sn)
    links = target_links.shape[0]
    width = feats.shape[0]
    barrier = greet(owners, me, n_sn)
    load = pltpu.make_async_copy(feats, points, own_sem.at[2])
    load.start()

    def choose(region, carry):
        def slot_at(k):
            return block_slot[target_block[region * targets + k]]

        block = named_block(me, targets, sn_blocks, target_count[region], slot_at)[1]
        block_of[region] = block
        rows = sn_positions[:, :BLOCK]
        for b in range(1, sn_blocks):
            rows = jnp.where(block == b, sn_positions[:, b * BLOCK : (b + 1) * BLOCK], rows)
        wanted[region] = rows
        return carry

    lax.fori_loop(0, owners, choose, 0)

    def slot_of(k, carry):
        slots[k] = block_slot[target_block[me * targets + k]]
        return carry

    lax.fori_loop(0, targets, slot_of, 0)
    my_count = target_count[me]

    def pos_copy(other, slot_at):
        return pltpu.make_async_remote_copy(
            src_ref=wanted.at[other],
            dst_ref=everywhere.at[slot_at],
            send_sem=pos_send.at[other],
            recv_sem=pos_recv.at[slot_at],
            device_id=peer(other, n_sn),
            device_id_type=MESH,
        )

    def start_pos(i, carry):
        pos_copy(lax.rem(me + far_first(i, owners), owners), me).start()
        return carry

    pl.semaphore_wait(barrier, owners - 1)
    lax.fori_loop(0, owners - 1, start_pos, 0)
    own_pos = pltpu.make_async_copy(wanted.at[me], everywhere.at[me], own_sem.at[0])
    own_pos.start()
    load.wait()

    def mlp(step, carry):
        span = pl.ds(pl.multiple_of(step * CHUNK, CHUNK), CHUNK)
        inner = jax.nn.gelu(contract(w_in[...], points[:, span], 0, 0)).astype(BF16)
        hid = contract(w_mid[...], inner, 0, 0).astype(BF16)
        places = positions[:, span]
        for q in range(CHUNK // BLOCK):
            hidden[step * (CHUNK // BLOCK) + q] = hid[:, q * BLOCK : (q + 1) * BLOCK]
            point_blocks[step * (CHUNK // BLOCK) + q] = places[:, q * BLOCK : (q + 1) * BLOCK]
        return carry

    lax.fori_loop(0, feats.shape[1] // CHUNK, mlp, 0)

    def msg_copy(other, slot_at):
        return pltpu.make_async_remote_copy(
            src_ref=outgoing.at[other],
            dst_ref=arrived.at[slot_at],
            send_sem=msg_send.at[other],
            recv_sem=msg_recv.at[slot_at],
            device_id=peer(other, n_sn),
            device_id_type=MESH,
        )

    def build(other):
        which, block, live = named_block(
            other, targets, sn_blocks, my_count, lambda k: slots[k]
        )
        sn_cols = columns_of(everywhere[other])
        kernels = []
        blocks = []
        for j in range(links):
            link = target_links[j, which]
            pts = point_blocks[link]
            dist = jnp.zeros((BLOCK, BLOCK), F32)
            for c in range(3):
                gap = sn_cols[:, c : c + 1] - pts[c : c + 1, :]
                dist = dist + gap * gap
            kernels.append(1.0 / (1.0 + dist * INV_RADIUS_SQ))
            blocks.append(hidden[link])
        total = kernels[0]
        for extra in kernels[1:]:
            total = total + extra
        total = jnp.sum(jnp.transpose(total), axis=0, keepdims=True)
        message = contract(
            jnp.concatenate(blocks, axis=1),
            jnp.concatenate([one.astype(BF16) for one in kernels], axis=1),
            1,
            1,
        )
        outgoing[other, :width, :] = (message * live).astype(BF16)
        outgoing[other, width:, :] = jnp.broadcast_to(total * live, (STAT_ROWS, BLOCK)).astype(BF16)

    def nth(i):
        return lax.rem(me + far_first(i, owners), owners)

    def build_next(i):
        pos_copy(nth(i), nth(i)).wait_recv()
        build(nth(i))

    build_next(0)

    def send(i, carry):
        build_next(i)
        msg_copy(nth(i - 1), me).start()
        return carry

    lax.fori_loop(1, owners - 1, send, 0)
    own_pos.wait()
    build(me)
    msg_copy(nth(owners - 2), me).start()
    own = pltpu.make_async_copy(outgoing.at[me], arrived.at[me], own_sem.at[1])
    own.start()
    own.wait()

    def add(source):
        block = block_of[source]
        message = arrived[source].astype(F32)
        for b in range(sn_blocks):
            sums[b] += jnp.where(block == b, message, 0.0)

    sums[...] = jnp.zeros_like(sums)
    add(me)

    def finish(i, carry):
        copy = msg_copy(nth(owners - 2 - i), nth(owners - 2 - i))
        copy.wait_recv()
        add(nth(owners - 2 - i))
        return carry

    lax.fori_loop(0, owners - 1, finish, 0)

    def sent(i, carry):
        msg_copy(nth(i), nth(i)).wait_send()
        pos_copy(nth(i), nth(i)).wait_send()
        return carry

    lax.fori_loop(0, owners - 1, sent, 0)
    for b in range(sn_blocks):
        scale = 1.0 / (1.0 + sums[b, width : width + 1, :])
        pooled[:, b * BLOCK : (b + 1) * BLOCK] = (sums[b, :width, :] * scale).astype(BF16)


def thirds(x):
    first = x.astype(BF16).astype(F32)
    second = (x - first).astype(BF16).astype(F32)
    third = x - first - second
    return [first, second, third]


def post_kernel(pooled, w_post, features_out):
    features_out[...] = jax.nn.gelu(contract(w_post[...], pooled[...], 0, 0)).astype(BF16)


def attend_kernel(
    owners,
    n_sn,
    features,
    queries,
    w_key,
    w_value,
    w_out,
    normed,
    values_t,
    keys,
    parts,
    arrived,
    send_sem,
    recv_sem,
    own_sem,
):
    me = place(n_sn)
    width, latents = queries.shape
    head_width = width // HEADS
    share = latents // owners
    chunks = latents // LATENT_CHUNK
    per_chunk = LATENT_CHUNK // share
    barrier = greet(owners, me, n_sn)
    keys[...] = contract(features[...], w_key[...], 0, 0).astype(BF16)
    values_t[...] = contract(w_value[...], features[...], 0, 0).astype(BF16)
    row_head = lax.broadcasted_iota(jnp.int32, (width, LATENT_CHUNK), 0) // head_width
    first = lax.div(me, per_chunk) + chunks // 2

    def attend(step, carry):
        chunk = lax.rem(first + step, chunks)
        at = pl.multiple_of(chunk * LATENT_CHUNK, LATENT_CHUNK)
        part = queries[:, pl.ds(at, LATENT_CHUNK)] * BF16(head_width ** (-0.5))
        outs, peaks, totals = [], [], []
        for h in range(HEADS):
            scores = contract(keys[...], jnp.where(row_head == h, part, BF16(0.0)), 1, 0)
            peak = jnp.max(scores, axis=0, keepdims=True)
            probs = jnp.exp(scores - peak)
            totals += thirds(jnp.sum(probs, axis=0, keepdims=True))
            peaks += thirds(peak)
            own_values = values_t[h * head_width : (h + 1) * head_width, :]
            outs.append(contract(own_values, probs.astype(BF16), 1, 0))
        pad = jnp.zeros((OUT_LANES - width - 6 * HEADS, LATENT_CHUNK), F32)
        whole = jnp.transpose(jnp.concatenate(outs + peaks + totals + [pad], axis=0))
        for j in range(per_chunk):
            parts[chunk * per_chunk + j] = whole[j * share : (j + 1) * share, :].astype(BF16)
        return carry

    def copy_of(other, slot_at):
        return pltpu.make_async_remote_copy(
            src_ref=parts.at[other],
            dst_ref=arrived.at[slot_at],
            send_sem=send_sem.at[other],
            recv_sem=recv_sem.at[slot_at],
            device_id=peer(other, n_sn),
            device_id_type=MESH,
        )

    def send_chunk(step):
        chunk = lax.rem(first + step, chunks)

        def start(j, carry):
            other = chunk * per_chunk + lax.rem(me + j, per_chunk)

            @pl.when(other != me)
            def _():
                copy_of(other, me).start()

            return carry

        lax.fori_loop(0, per_chunk, start, 0)

    attend(0, 0)
    pl.semaphore_wait(barrier, owners - 1)

    def step_on(step, carry):
        send_chunk(step - 1)
        return attend(step, carry)

    lax.fori_loop(1, chunks, step_on, 0)
    send_chunk(chunks - 1)
    own = pltpu.make_async_copy(parts.at[me], arrived.at[me], own_sem)
    own.start()
    own.wait()

    def finish(off, carry):
        other = lax.rem(me + off, owners)
        copy = copy_of(other, other)
        copy.wait_send()
        copy.wait_recv()
        return carry

    lax.fori_loop(1, owners, finish, 0)
    lane = lax.broadcasted_iota(jnp.int32, (OUT_LANES, width), 0) - width
    head_of = lax.broadcasted_iota(jnp.int32, (OUT_LANES, width), 1) // head_width
    is_peak = jnp.logical_and(lane >= 3 * head_of, lane < 3 * head_of + 3)
    total_lane = lane - 3 * HEADS
    is_total = jnp.logical_and(total_lane >= 3 * head_of, total_lane < 3 * head_of + 3)
    flat = jnp.concatenate([arrived[source] for source in range(owners)], axis=0)
    peaks = contract(flat, jnp.where(is_peak, 1.0, 0.0).astype(BF16), 1, 0)
    totals = contract(flat, jnp.where(is_total, 1.0, 0.0).astype(BF16), 1, 0)

    def of(full, source):
        return full[source * share : (source + 1) * share, :]

    top = of(peaks, 0)
    for source in range(1, owners):
        top = jnp.maximum(top, of(peaks, source))
    output = jnp.zeros((share, width), F32)
    total = jnp.zeros((share, width), F32)
    for source in range(owners):
        scale = jnp.exp(of(peaks, source) - top)
        output = output + scale * arrived[source][:, :width].astype(F32)
        total = total + scale * of(totals, source)
    attended = (output / total).astype(BF16)
    projected = jnp.dot(attended, w_out[...], preferred_element_type=F32)
    mean_sq = jnp.mean(projected * projected, axis=-1, keepdims=True)
    normed[...] = projected * lax.rsqrt(mean_sq + 1e-06)


def per_device(
    n_sn,
    owners,
    point_features,
    point_positions,
    sn_positions,
    latent_queries,
    target_block,
    target_links,
    target_count,
    block_slot,
    w_in,
    w_mid,
    w_post,
    w_key,
    w_value,
    w_out,
    out_gain,
):
    targets = target_links.shape[0]
    width = point_features.shape[1]
    sn_rows = sn_positions.shape[1]
    sn_blocks = sn_rows // BLOCK
    latents = latent_queries.shape[0]
    share = latents // owners
    smem = pl.BlockSpec(memory_space=pltpu.SMEM)
    vmem = pl.BlockSpec(memory_space=pltpu.VMEM)
    hbm = pl.BlockSpec(memory_space=pl.ANY)
    dma = pltpu.SemaphoreType.DMA
    pooled = pl.pallas_call(
        functools.partial(message_kernel, owners, n_sn, sn_blocks, targets),
        out_shape=jax.ShapeDtypeStruct((width, sn_rows), BF16),
        in_specs=[smem] * 4 + [hbm] + [vmem] * 4,
        out_specs=vmem,
        scratch_shapes=[
            pltpu.VMEM((owners, width + STAT_ROWS, BLOCK), BF16),
            pltpu.VMEM((sn_blocks, width + STAT_ROWS, BLOCK), F32),
            pltpu.SMEM((owners,), jnp.int32),
            pltpu.VMEM(point_features.shape[::-1], BF16),
            pltpu.VMEM((owners, 3, BLOCK), F32),
            pltpu.VMEM((owners, 3, BLOCK), F32),
            pltpu.VMEM((point_features.shape[0] // BLOCK, width, BLOCK), BF16),
            pltpu.VMEM((point_features.shape[0] // BLOCK, 3, BLOCK), F32),
            pltpu.VMEM((owners, width + STAT_ROWS, BLOCK), BF16),
            pltpu.SMEM((targets,), jnp.int32),
            dma((owners,)),
            dma((owners,)),
            dma((owners,)),
            dma((owners,)),
            dma((3,)),
        ],
        compiler_params=pltpu.CompilerParams(collective_id=0, has_side_effects=True),
        name="messages",
    )(
        target_block,
        target_links.T,
        target_count,
        block_slot,
        point_features.T,
        point_positions,
        sn_positions,
        w_in,
        w_mid,
    )
    features_t = pl.pallas_call(
        post_kernel,
        out_shape=jax.ShapeDtypeStruct((width, sn_rows), BF16),
        in_specs=[vmem] * 2,
        out_specs=vmem,
        name="post",
    )(pooled, w_post)
    normed = pl.pallas_call(
        functools.partial(attend_kernel, owners, n_sn),
        out_shape=jax.ShapeDtypeStruct((share, width), F32),
        in_specs=[vmem] * 5,
        out_specs=vmem,
        scratch_shapes=[
            pltpu.VMEM((width, sn_rows), BF16),
            pltpu.VMEM((sn_rows, width), BF16),
            pltpu.VMEM((owners, share, OUT_LANES), BF16),
            pltpu.VMEM((owners, share, OUT_LANES), BF16),
            dma((owners,)),
            dma((owners,)),
            dma,
        ],
        compiler_params=pltpu.CompilerParams(collective_id=1, has_side_effects=True),
        name="attend",
    )(features_t, latent_queries.T, w_key, w_value, w_out)
    return (features_t.T, (normed * out_gain).astype(BF16))


def solution(mesh):
    n_sn = mesh.shape["sn"]
    owners = mesh.shape["pts"] * n_sn
    everything = ("groups", "pts", "sn")
    in_specs = (
        P(everything, None),
        P(None, everything),
        P(None, everything),
        P(),
        P("groups"),
        P(everything, None),
        P("groups"),
        P("groups"),
        P(),
        P(),
        P(),
        P(),
        P(),
        P(),
        P(),
    )
    out_specs = (P(everything, None), P(everything, None))
    return jax.shard_map(
        functools.partial(per_device, n_sn, owners),
        mesh=mesh,
        in_specs=in_specs,
        out_specs=out_specs,
        check_vma=False,
    )
```

```python
import functools

import jax
import jax.numpy as jnp
from jax import lax
from jax.experimental import pallas as pl
from jax.experimental.pallas import tpu as pltpu
from jax.sharding import PartitionSpec as P

HEADS = 3
BLOCK = 128
INV_RADIUS_SQ = 100.0
MESH = pl.DeviceIdType.MESH
STAT_ROWS = 8
CHUNK = 512
LATENT_CHUNK = 256
OUT_LANES = 256
F32 = jnp.float32
BF16 = jnp.bfloat16


def contract(a, b, dim_a, dim_b):
    return lax.dot_general(a, b, (((dim_a,), (dim_b,)), ((), ())), preferred_element_type=F32)


def place(n_sn):
    return lax.axis_index("pts") * n_sn + lax.axis_index("sn")


def peer(index, n_sn):
    return {"pts": lax.div(index, n_sn), "sn": lax.rem(index, n_sn)}


def greet(owners, me, n_sn):
    barrier = pltpu.get_barrier_semaphore()

    def signal(off, carry):
        other = lax.rem(me + off, owners)
        pl.semaphore_signal(barrier, inc=1, device_id=peer(other, n_sn), device_id_type=MESH)
        return carry

    lax.fori_loop(1, owners, signal, 0)
    return barrier


def far_first(i, owners):
    return owners // 2 + lax.div(i + 1, 2) * (2 * lax.rem(i + 1, 2) - 1)


def named_block(owner, targets, sn_blocks, count, slot_at):
    def look(k, state):
        which, block, live = state
        slot = slot_at(k)
        hit = jnp.logical_and(lax.div(slot, sn_blocks) == owner, k < count)
        return (
            jnp.where(hit, k, which),
            jnp.where(hit, lax.rem(slot, sn_blocks), block),
            jnp.where(hit, 1.0, live),
        )

    start = (jnp.int32(0), jnp.int32(0), F32(0.0))
    return lax.fori_loop(0, targets, look, start, unroll=targets <= 8)


def columns_of(rows):
    padded = jnp.concatenate([rows, jnp.zeros((5, rows.shape[1]), F32)], axis=0)
    return jnp.transpose(padded)


def thirds(x):
    first = x.astype(BF16).astype(F32)
    second = (x - first).astype(BF16).astype(F32)
    third = x - first - second
    return [first, second, third]


def encoder_kernel(
    owners,
    n_sn,
    sn_blocks,
    targets,
    target_block,
    target_links,
    target_count,
    block_slot,
    feats,
    positions,
    sn_positions,
    w_in,
    w_mid,
    w_post,
    queries,
    w_key,
    w_value,
    w_out,
    features,
    normed,
    pooled,
    values_t,
    keys,
    parts,
    landed,
    part_send,
    part_recv,
    arrived,
    sums,
    block_of,
    points,
    wanted,
    everywhere,
    hidden,
    point_blocks,
    outgoing,
    slots,
    pos_send,
    pos_recv,
    msg_send,
    msg_recv,
    own_sem,
):
    me = place(n_sn)
    links = target_links.shape[0]
    width = feats.shape[0]
    barrier = greet(owners, me, n_sn)
    load = pltpu.make_async_copy(feats, points, own_sem.at[2])
    load.start()

    def choose(region, carry):
        def slot_at(k):
            return block_slot[target_block[region * targets + k]]

        block = named_block(me, targets, sn_blocks, target_count[region], slot_at)[1]
        block_of[region] = block
        rows = sn_positions[:, :BLOCK]
        for b in range(1, sn_blocks):
            rows = jnp.where(block == b, sn_positions[:, b * BLOCK : (b + 1) * BLOCK], rows)
        wanted[region] = rows
        return carry

    lax.fori_loop(0, owners, choose, 0)

    def slot_of(k, carry):
        slots[k] = block_slot[target_block[me * targets + k]]
        return carry

    lax.fori_loop(0, targets, slot_of, 0)
    my_count = target_count[me]

    def pos_copy(other, slot_at):
        return pltpu.make_async_remote_copy(
            src_ref=wanted.at[other],
            dst_ref=everywhere.at[slot_at],
            send_sem=pos_send.at[other],
            recv_sem=pos_recv.at[slot_at],
            device_id=peer(other, n_sn),
            device_id_type=MESH,
        )

    def start_pos(i, carry):
        pos_copy(lax.rem(me + far_first(i, owners), owners), me).start()
        return carry

    pl.semaphore_wait(barrier, owners - 1)
    lax.fori_loop(0, owners - 1, start_pos, 0)
    own_pos = pltpu.make_async_copy(wanted.at[me], everywhere.at[me], own_sem.at[0])
    own_pos.start()
    load.wait()

    def mlp(step, carry):
        span = pl.ds(pl.multiple_of(step * CHUNK, CHUNK), CHUNK)
        inner = jax.nn.gelu(contract(w_in[...], points[:, span], 0, 0)).astype(BF16)
        hid = contract(w_mid[...], inner, 0, 0).astype(BF16)
        places = positions[:, span]
        for q in range(CHUNK // BLOCK):
            hidden[step * (CHUNK // BLOCK) + q] = hid[:, q * BLOCK : (q + 1) * BLOCK]
            point_blocks[step * (CHUNK // BLOCK) + q] = places[:, q * BLOCK : (q + 1) * BLOCK]
        return carry

    lax.fori_loop(0, feats.shape[1] // CHUNK, mlp, 0)

    def msg_copy(other, slot_at):
        return pltpu.make_async_remote_copy(
            src_ref=outgoing.at[other],
            dst_ref=arrived.at[slot_at],
            send_sem=msg_send.at[other],
            recv_sem=msg_recv.at[slot_at],
            device_id=peer(other, n_sn),
            device_id_type=MESH,
        )

    def build(other):
        which, block, live = named_block(
            other, targets, sn_blocks, my_count, lambda k: slots[k]
        )
        sn_cols = columns_of(everywhere[other])
        kernels = []
        blocks = []
        for j in range(links):
            link = target_links[j, which]
            pts = point_blocks[link]
            dist = jnp.zeros((BLOCK, BLOCK), F32)
            for c in range(3):
                gap = sn_cols[:, c : c + 1] - pts[c : c + 1, :]
                dist = dist + gap * gap
            kernels.append(1.0 / (1.0 + dist * INV_RADIUS_SQ))
            blocks.append(hidden[link])
        total = kernels[0]
        for extra in kernels[1:]:
            total = total + extra
        total = jnp.sum(jnp.transpose(total), axis=0, keepdims=True)
        message = contract(
            jnp.concatenate(blocks, axis=1),
            jnp.concatenate([one.astype(BF16) for one in kernels], axis=1),
            1,
            1,
        )
        outgoing[other, :width, :] = (message * live).astype(BF16)
        outgoing[other, width:, :] = jnp.broadcast_to(total * live, (STAT_ROWS, BLOCK)).astype(BF16)

    def nth(i):
        return lax.rem(me + far_first(i, owners), owners)

    def build_next(i):
        pos_copy(nth(i), nth(i)).wait_recv()
        build(nth(i))

    build_next(0)

    def send(i, carry):
        build_next(i)
        msg_copy(nth(i - 1), me).start()
        return carry

    lax.fori_loop(1, owners - 1, send, 0)
    own_pos.wait()
    build(me)
    msg_copy(nth(owners - 2), me).start()
    def add(source, message):
        block = block_of[source]
        for b in range(sn_blocks):
            sums[b] += jnp.where(block == b, message, 0.0)

    sums[...] = jnp.zeros_like(sums)
    add(me, outgoing[me].astype(F32))

    def finish(i, carry):
        source = nth(lax.rem(i + owners // 2 + 1, owners - 1))
        msg_copy(source, source).wait_recv()
        add(source, arrived[source].astype(F32))
        return carry

    lax.fori_loop(0, owners - 1, finish, 0)

    def sent(i, carry):
        msg_copy(nth(i), nth(i)).wait_send()
        pos_copy(nth(i), nth(i)).wait_send()
        return carry

    lax.fori_loop(0, owners - 1, sent, 0)
    for b in range(sn_blocks):
        scale = 1.0 / (1.0 + sums[b, width : width + 1, :])
        pooled[:, b * BLOCK : (b + 1) * BLOCK] = (sums[b, :width, :] * scale).astype(BF16)


    head_width = width // HEADS
    latents = queries.shape[1]
    share = latents // owners
    chunks = latents // LATENT_CHUNK
    per_chunk = LATENT_CHUNK // share
    features[...] = jax.nn.gelu(contract(w_post[...], pooled[...], 0, 0)).astype(BF16)
    keys[...] = contract(features[...], w_key[...], 0, 0).astype(BF16)
    values_t[...] = contract(w_value[...], features[...], 0, 0).astype(BF16)
    row_head = lax.broadcasted_iota(jnp.int32, (width, LATENT_CHUNK), 0) // head_width
    first = lax.div(me, per_chunk) + chunks // 2

    def attend(step, carry):
        chunk = lax.rem(first + step, chunks)
        at = pl.multiple_of(chunk * LATENT_CHUNK, LATENT_CHUNK)
        part = queries[:, pl.ds(at, LATENT_CHUNK)] * BF16(head_width ** (-0.5))
        outs, peaks, totals = [], [], []
        for h in range(HEADS):
            scores = contract(keys[...], jnp.where(row_head == h, part, BF16(0.0)), 1, 0)
            peak = jnp.max(scores, axis=0, keepdims=True)
            probs = jnp.exp(scores - peak)
            totals += thirds(jnp.sum(probs, axis=0, keepdims=True))
            peaks += thirds(peak)
            own_values = values_t[h * head_width : (h + 1) * head_width, :]
            outs.append(contract(own_values, probs.astype(BF16), 1, 0))
        pad = jnp.zeros((OUT_LANES - width - 6 * HEADS, LATENT_CHUNK), F32)
        whole = jnp.transpose(jnp.concatenate(outs + peaks + totals + [pad], axis=0))
        for j in range(per_chunk):
            parts[chunk * per_chunk + j] = whole[j * share : (j + 1) * share, :].astype(BF16)
        return carry

    def copy_of(other, slot_at):
        return pltpu.make_async_remote_copy(
            src_ref=parts.at[other],
            dst_ref=landed.at[slot_at],
            send_sem=part_send.at[other],
            recv_sem=part_recv.at[slot_at],
            device_id=peer(other, n_sn),
            device_id_type=MESH,
        )

    def send_chunk(step):
        chunk = lax.rem(first + step, chunks)

        def start(j, carry):
            other = chunk * per_chunk + lax.rem(me + j, per_chunk)

            @pl.when(other != me)
            def _():
                copy_of(other, me).start()

            return carry

        lax.fori_loop(0, per_chunk, start, 0)

    attend(0, 0)

    def step_on(step, carry):
        send_chunk(step - 1)
        return attend(step, carry)

    lax.fori_loop(1, chunks, step_on, 0)
    send_chunk(chunks - 1)
    own = pltpu.make_async_copy(parts.at[me], landed.at[me], own_sem.at[1])
    own.start()
    own.wait()

    def settle(off, carry):
        other = lax.rem(me + off, owners)
        copy = copy_of(other, other)
        copy.wait_send()
        copy.wait_recv()
        return carry

    lax.fori_loop(1, owners, settle, 0)
    lane = lax.broadcasted_iota(jnp.int32, (OUT_LANES, width), 0) - width
    head_of = lax.broadcasted_iota(jnp.int32, (OUT_LANES, width), 1) // head_width
    is_peak = jnp.logical_and(lane >= 3 * head_of, lane < 3 * head_of + 3)
    total_lane = lane - 3 * HEADS
    is_total = jnp.logical_and(total_lane >= 3 * head_of, total_lane < 3 * head_of + 3)
    flat = jnp.concatenate([landed[source] for source in range(owners)], axis=0)
    peaks = contract(flat, jnp.where(is_peak, 1.0, 0.0).astype(BF16), 1, 0)
    totals = contract(flat, jnp.where(is_total, 1.0, 0.0).astype(BF16), 1, 0)

    def of(full, source):
        return full[source * share : (source + 1) * share, :]

    top = of(peaks, 0)
    for source in range(1, owners):
        top = jnp.maximum(top, of(peaks, source))
    output = jnp.zeros((share, width), F32)
    total = jnp.zeros((share, width), F32)
    for source in range(owners):
        scale = jnp.exp(of(peaks, source) - top)
        output = output + scale * landed[source][:, :width].astype(F32)
        total = total + scale * of(totals, source)
    attended = (output / total).astype(BF16)
    projected = jnp.dot(attended, w_out[...], preferred_element_type=F32)
    mean_sq = jnp.mean(projected * projected, axis=-1, keepdims=True)
    normed[...] = projected * lax.rsqrt(mean_sq + 1e-06)


def per_device(
    n_sn,
    owners,
    point_features,
    point_positions,
    sn_positions,
    latent_queries,
    target_block,
    target_links,
    target_count,
    block_slot,
    w_in,
    w_mid,
    w_post,
    w_key,
    w_value,
    w_out,
    out_gain,
):
    targets = target_links.shape[0]
    width = point_features.shape[1]
    sn_rows = sn_positions.shape[1]
    sn_blocks = sn_rows // BLOCK
    latents = latent_queries.shape[0]
    share = latents // owners
    smem = pl.BlockSpec(memory_space=pltpu.SMEM)
    vmem = pl.BlockSpec(memory_space=pltpu.VMEM)
    hbm = pl.BlockSpec(memory_space=pl.ANY)
    dma = pltpu.SemaphoreType.DMA
    features_t, normed = pl.pallas_call(
        functools.partial(encoder_kernel, owners, n_sn, sn_blocks, targets),
        out_shape=(
            jax.ShapeDtypeStruct((width, sn_rows), BF16),
            jax.ShapeDtypeStruct((share, width), F32),
        ),
        in_specs=[smem] * 4 + [hbm] + [vmem] * 9,
        out_specs=(vmem, vmem),
        scratch_shapes=[
            pltpu.VMEM((width, sn_rows), BF16),
            pltpu.VMEM((width, sn_rows), BF16),
            pltpu.VMEM((sn_rows, width), BF16),
            pltpu.VMEM((owners, share, OUT_LANES), BF16),
            pltpu.VMEM((owners, share, OUT_LANES), BF16),
            dma((owners,)),
            dma((owners,)),
            pltpu.VMEM((owners, width + STAT_ROWS, BLOCK), BF16),
            pltpu.VMEM((sn_blocks, width + STAT_ROWS, BLOCK), F32),
            pltpu.SMEM((owners,), jnp.int32),
            pltpu.VMEM(point_features.shape[::-1], BF16),
            pltpu.VMEM((owners, 3, BLOCK), F32),
            pltpu.VMEM((owners, 3, BLOCK), F32),
            pltpu.VMEM((point_features.shape[0] // BLOCK, width, BLOCK), BF16),
            pltpu.VMEM((point_features.shape[0] // BLOCK, 3, BLOCK), F32),
            pltpu.VMEM((owners, width + STAT_ROWS, BLOCK), BF16),
            pltpu.SMEM((targets,), jnp.int32),
            dma((owners,)),
            dma((owners,)),
            dma((owners,)),
            dma((owners,)),
            dma((3,)),
        ],
        compiler_params=pltpu.CompilerParams(collective_id=0, has_side_effects=True),
        name="encoder",
    )(
        target_block,
        target_links.T,
        target_count,
        block_slot,
        point_features.T,
        point_positions,
        sn_positions,
        w_in,
        w_mid,
        w_post,
        latent_queries.T,
        w_key,
        w_value,
        w_out,
    )
    return (features_t.T, (normed * out_gain).astype(BF16))


def solution(mesh):
    n_sn = mesh.shape["sn"]
    owners = mesh.shape["pts"] * n_sn
    everything = ("groups", "pts", "sn")
    in_specs = (
        P(everything, None),
        P(None, everything),
        P(None, everything),
        P(),
        P("groups"),
        P(everything, None),
        P("groups"),
        P("groups"),
        P(),
        P(),
        P(),
        P(),
        P(),
        P(),
        P(),
    )
    out_specs = (P(everything, None), P(everything, None))
    return jax.shard_map(
        functools.partial(per_device, n_sn, owners),
        mesh=mesh,
        in_specs=in_specs,
        out_specs=out_specs,
        check_vma=False,
    )
```

```python
import functools

import jax
import jax.numpy as jnp
from jax import lax
from jax.experimental import pallas as pl
from jax.experimental.pallas import tpu as pltpu
from jax.sharding import PartitionSpec as P

HEADS = 3
BLOCK = 128
INV_RADIUS_SQ = 100.0
MESH = pl.DeviceIdType.MESH
STAT_ROWS = 8
CHUNK = 1024
LATENT_CHUNK = 256
OUT_LANES = 256
F32 = jnp.float32
BF16 = jnp.bfloat16


def contract(a, b, dim_a, dim_b):
    return lax.dot_general(a, b, (((dim_a,), (dim_b,)), ((), ())), preferred_element_type=F32)


def place(n_sn):
    return lax.axis_index("pts") * n_sn + lax.axis_index("sn")


def peer(index, n_sn):
    return {"pts": lax.div(index, n_sn), "sn": lax.rem(index, n_sn)}


def greet(owners, me, n_sn):
    barrier = pltpu.get_barrier_semaphore()

    def signal(off, carry):
        other = lax.rem(me + off, owners)
        pl.semaphore_signal(barrier, inc=1, device_id=peer(other, n_sn), device_id_type=MESH)
        return carry

    lax.fori_loop(1, owners, signal, 0)
    return barrier


def far_first(i, owners):
    return owners // 2 + lax.div(i + 1, 2) * (2 * lax.rem(i + 1, 2) - 1)


def named_block(owner, targets, sn_blocks, count, slot_at):
    def look(k, state):
        which, block, live = state
        slot = slot_at(k)
        hit = jnp.logical_and(lax.div(slot, sn_blocks) == owner, k < count)
        return (
            jnp.where(hit, k, which),
            jnp.where(hit, lax.rem(slot, sn_blocks), block),
            jnp.where(hit, 1.0, live),
        )

    start = (jnp.int32(0), jnp.int32(0), F32(0.0))
    return lax.fori_loop(0, targets, look, start, unroll=targets <= 8)


def columns_of(rows):
    padded = jnp.concatenate([rows, jnp.zeros((5, rows.shape[1]), F32)], axis=0)
    return jnp.transpose(padded)


def thirds(x):
    first = x.astype(BF16).astype(F32)
    second = (x - first).astype(BF16).astype(F32)
    third = x - first - second
    return [first, second, third]


def encoder_kernel(
    owners,
    n_sn,
    sn_blocks,
    targets,
    target_block,
    target_links,
    target_count,
    block_slot,
    feats,
    positions,
    sn_positions,
    w_in,
    w_mid,
    w_post,
    queries,
    w_key,
    w_value,
    w_out,
    features,
    normed,
    pooled,
    values_t,
    keys,
    parts,
    landed,
    part_send,
    part_recv,
    arrived,
    sums,
    block_of,
    points,
    wanted,
    everywhere,
    hidden,
    point_blocks,
    outgoing,
    slots,
    pos_send,
    pos_recv,
    msg_send,
    msg_recv,
    own_sem,
):
    me = place(n_sn)
    links = target_links.shape[0]
    width = feats.shape[0]
    barrier = greet(owners, me, n_sn)
    load = pltpu.make_async_copy(feats, points, own_sem.at[2])
    load.start()

    def choose(region, carry):
        def slot_at(k):
            return block_slot[target_block[region * targets + k]]

        block = named_block(me, targets, sn_blocks, target_count[region], slot_at)[1]
        block_of[region] = block
        rows = sn_positions[:, :BLOCK]
        for b in range(1, sn_blocks):
            rows = jnp.where(block == b, sn_positions[:, b * BLOCK : (b + 1) * BLOCK], rows)
        wanted[region] = rows
        return carry

    lax.fori_loop(0, owners, choose, 0)

    def slot_of(k, carry):
        slots[k] = block_slot[target_block[me * targets + k]]
        return carry

    lax.fori_loop(0, targets, slot_of, 0)
    my_count = target_count[me]

    def pos_copy(other, slot_at):
        return pltpu.make_async_remote_copy(
            src_ref=wanted.at[other],
            dst_ref=everywhere.at[slot_at],
            send_sem=pos_send.at[other],
            recv_sem=pos_recv.at[slot_at],
            device_id=peer(other, n_sn),
            device_id_type=MESH,
        )

    def start_pos(i, carry):
        pos_copy(lax.rem(me + far_first(i, owners), owners), me).start()
        return carry

    pl.semaphore_wait(barrier, owners - 1)
    lax.fori_loop(0, owners - 1, start_pos, 0)
    own_pos = pltpu.make_async_copy(wanted.at[me], everywhere.at[me], own_sem.at[0])
    own_pos.start()
    load.wait()

    def mlp(step, carry):
        span = pl.ds(pl.multiple_of(step * CHUNK, CHUNK), CHUNK)
        inner = jax.nn.gelu(contract(w_in[...], points[:, span], 0, 0)).astype(BF16)
        hid = contract(w_mid[...], inner, 0, 0).astype(BF16)
        places = positions[:, span]
        for q in range(CHUNK // BLOCK):
            hidden[step * (CHUNK // BLOCK) + q] = hid[:, q * BLOCK : (q + 1) * BLOCK]
            point_blocks[step * (CHUNK // BLOCK) + q] = places[:, q * BLOCK : (q + 1) * BLOCK]
        return carry

    lax.fori_loop(0, feats.shape[1] // CHUNK, mlp, 0)

    def msg_copy(other, slot_at):
        return pltpu.make_async_remote_copy(
            src_ref=outgoing.at[other],
            dst_ref=arrived.at[slot_at],
            send_sem=msg_send.at[other],
            recv_sem=msg_recv.at[slot_at],
            device_id=peer(other, n_sn),
            device_id_type=MESH,
        )

    def build(other):
        which, block, live = named_block(
            other, targets, sn_blocks, my_count, lambda k: slots[k]
        )
        sn_cols = columns_of(everywhere[other])
        kernels = []
        blocks = []
        for j in range(links):
            link = target_links[j, which]
            pts = point_blocks[link]
            dist = jnp.zeros((BLOCK, BLOCK), F32)
            for c in range(3):
                gap = sn_cols[:, c : c + 1] - pts[c : c + 1, :]
                dist = dist + gap * gap
            kernels.append(1.0 / (1.0 + dist * INV_RADIUS_SQ))
            blocks.append(hidden[link])
        total = kernels[0]
        for extra in kernels[1:]:
            total = total + extra
        total = jnp.sum(jnp.transpose(total), axis=0, keepdims=True)
        message = contract(
            jnp.concatenate(blocks, axis=1),
            jnp.concatenate([one.astype(BF16) for one in kernels], axis=1),
            1,
            1,
        )
        outgoing[other, :width, :] = (message * live).astype(BF16)
        outgoing[other, width:, :] = jnp.broadcast_to(total * live, (STAT_ROWS, BLOCK)).astype(BF16)

    def nth(i):
        return lax.rem(me + far_first(i, owners), owners)

    def build_next(i):
        pos_copy(nth(i), nth(i)).wait_recv()
        build(nth(i))

    build_next(0)

    def send(i, carry):
        build_next(i)
        msg_copy(nth(i - 1), me).start()
        return carry

    lax.fori_loop(1, owners - 1, send, 0)
    own_pos.wait()
    build(me)
    msg_copy(nth(owners - 2), me).start()
    def add(source, message):
        block = block_of[source]
        for b in range(sn_blocks):
            sums[b] += jnp.where(block == b, message, 0.0)

    sums[...] = jnp.zeros_like(sums)
    add(me, outgoing[me].astype(F32))

    def finish(i, carry):
        source = nth(lax.rem(i + owners // 2 + 1, owners - 1))
        msg_copy(source, source).wait_recv()
        add(source, arrived[source].astype(F32))
        return carry

    lax.fori_loop(0, owners - 1, finish, 0)

    def sent(i, carry):
        msg_copy(nth(i), nth(i)).wait_send()
        pos_copy(nth(i), nth(i)).wait_send()
        return carry

    lax.fori_loop(0, owners - 1, sent, 0)
    for b in range(sn_blocks):
        scale = 1.0 / (1.0 + sums[b, width : width + 1, :])
        pooled[:, b * BLOCK : (b + 1) * BLOCK] = (sums[b, :width, :] * scale).astype(BF16)


    head_width = width // HEADS
    latents = queries.shape[1]
    share = latents // owners
    chunks = latents // LATENT_CHUNK
    per_chunk = LATENT_CHUNK // share
    features[...] = jax.nn.gelu(contract(w_post[...], pooled[...], 0, 0)).astype(BF16)
    keys[...] = contract(features[...], w_key[...], 0, 0).astype(BF16)
    values_t[...] = contract(w_value[...], features[...], 0, 0).astype(BF16)
    row_head = lax.broadcasted_iota(jnp.int32, (width, LATENT_CHUNK), 0) // head_width
    first = lax.div(me, per_chunk) + chunks // 2

    def attend(step, carry):
        chunk = lax.rem(first + step, chunks)
        at = pl.multiple_of(chunk * LATENT_CHUNK, LATENT_CHUNK)
        part = queries[:, pl.ds(at, LATENT_CHUNK)] * BF16(head_width ** (-0.5))
        outs, peaks, totals = [], [], []
        for h in range(HEADS):
            scores = contract(keys[...], jnp.where(row_head == h, part, BF16(0.0)), 1, 0)
            peak = jnp.max(scores, axis=0, keepdims=True)
            probs = jnp.exp(scores - peak)
            totals += thirds(jnp.sum(probs, axis=0, keepdims=True))
            peaks += thirds(peak)
            own_values = values_t[h * head_width : (h + 1) * head_width, :]
            outs.append(contract(own_values, probs.astype(BF16), 1, 0))
        pad = jnp.zeros((OUT_LANES - width - 6 * HEADS, LATENT_CHUNK), F32)
        whole = jnp.transpose(jnp.concatenate(outs + peaks + totals + [pad], axis=0))
        for j in range(per_chunk):
            parts[chunk * per_chunk + j] = whole[j * share : (j + 1) * share, :].astype(BF16)
        return carry

    def copy_of(other, slot_at):
        return pltpu.make_async_remote_copy(
            src_ref=parts.at[other],
            dst_ref=landed.at[slot_at],
            send_sem=part_send.at[other],
            recv_sem=part_recv.at[slot_at],
            device_id=peer(other, n_sn),
            device_id_type=MESH,
        )

    def send_chunk(step):
        chunk = lax.rem(first + step, chunks)

        def start(j, carry):
            other = chunk * per_chunk + lax.rem(me + j, per_chunk)

            @pl.when(other != me)
            def _():
                copy_of(other, me).start()

            return carry

        lax.fori_loop(0, per_chunk, start, 0)

    attend(0, 0)

    def step_on(step, carry):
        send_chunk(step - 1)
        return attend(step, carry)

    lax.fori_loop(1, chunks, step_on, 0)
    send_chunk(chunks - 1)
    own = pltpu.make_async_copy(parts.at[me], landed.at[me], own_sem.at[1])
    own.start()
    own.wait()

    def settle(off, carry):
        other = lax.rem(me + off, owners)
        copy = copy_of(other, other)
        copy.wait_send()
        copy.wait_recv()
        return carry

    lax.fori_loop(1, owners, settle, 0)
    lane = lax.broadcasted_iota(jnp.int32, (OUT_LANES, width), 0) - width
    head_of = lax.broadcasted_iota(jnp.int32, (OUT_LANES, width), 1) // head_width
    is_peak = jnp.logical_and(lane >= 3 * head_of, lane < 3 * head_of + 3)
    total_lane = lane - 3 * HEADS
    is_total = jnp.logical_and(total_lane >= 3 * head_of, total_lane < 3 * head_of + 3)
    flat = jnp.concatenate([landed[source] for source in range(owners)], axis=0)
    peaks = contract(flat, jnp.where(is_peak, 1.0, 0.0).astype(BF16), 1, 0)
    totals = contract(flat, jnp.where(is_total, 1.0, 0.0).astype(BF16), 1, 0)

    def of(full, source):
        return full[source * share : (source + 1) * share, :]

    top = of(peaks, 0)
    for source in range(1, owners):
        top = jnp.maximum(top, of(peaks, source))
    output = jnp.zeros((share, width), F32)
    total = jnp.zeros((share, width), F32)
    for source in range(owners):
        scale = jnp.exp(of(peaks, source) - top)
        output = output + scale * landed[source][:, :width].astype(F32)
        total = total + scale * of(totals, source)
    attended = (output / total).astype(BF16)
    projected = jnp.dot(attended, w_out[...], preferred_element_type=F32)
    mean_sq = jnp.mean(projected * projected, axis=-1, keepdims=True)
    normed[...] = projected * lax.rsqrt(mean_sq + 1e-06)


def per_device(
    n_sn,
    owners,
    point_features,
    point_positions,
    sn_positions,
    latent_queries,
    target_block,
    target_links,
    target_count,
    block_slot,
    w_in,
    w_mid,
    w_post,
    w_key,
    w_value,
    w_out,
    out_gain,
):
    targets = target_links.shape[0]
    width = point_features.shape[1]
    sn_rows = sn_positions.shape[1]
    sn_blocks = sn_rows // BLOCK
    latents = latent_queries.shape[0]
    share = latents // owners
    smem = pl.BlockSpec(memory_space=pltpu.SMEM)
    vmem = pl.BlockSpec(memory_space=pltpu.VMEM)
    hbm = pl.BlockSpec(memory_space=pl.ANY)
    dma = pltpu.SemaphoreType.DMA
    features_t, normed = pl.pallas_call(
        functools.partial(encoder_kernel, owners, n_sn, sn_blocks, targets),
        out_shape=(
            jax.ShapeDtypeStruct((width, sn_rows), BF16),
            jax.ShapeDtypeStruct((share, width), F32),
        ),
        in_specs=[smem] * 4 + [hbm] + [vmem] * 9,
        out_specs=(vmem, vmem),
        scratch_shapes=[
            pltpu.VMEM((width, sn_rows), BF16),
            pltpu.VMEM((width, sn_rows), BF16),
            pltpu.VMEM((sn_rows, width), BF16),
            pltpu.VMEM((owners, share, OUT_LANES), BF16),
            pltpu.VMEM((owners, share, OUT_LANES), BF16),
            dma((owners,)),
            dma((owners,)),
            pltpu.VMEM((owners, width + STAT_ROWS, BLOCK), BF16),
            pltpu.VMEM((sn_blocks, width + STAT_ROWS, BLOCK), F32),
            pltpu.SMEM((owners,), jnp.int32),
            pltpu.VMEM(point_features.shape[::-1], BF16),
            pltpu.VMEM((owners, 3, BLOCK), F32),
            pltpu.VMEM((owners, 3, BLOCK), F32),
            pltpu.VMEM((point_features.shape[0] // BLOCK, width, BLOCK), BF16),
            pltpu.VMEM((point_features.shape[0] // BLOCK, 3, BLOCK), F32),
            pltpu.VMEM((owners, width + STAT_ROWS, BLOCK), BF16),
            pltpu.SMEM((targets,), jnp.int32),
            dma((owners,)),
            dma((owners,)),
            dma((owners,)),
            dma((owners,)),
            dma((3,)),
        ],
        compiler_params=pltpu.CompilerParams(collective_id=0, has_side_effects=True),
        name="encoder",
    )(
        target_block,
        target_links.T,
        target_count,
        block_slot,
        point_features.T,
        point_positions,
        sn_positions,
        w_in,
        w_mid,
        w_post,
        latent_queries.T,
        w_key,
        w_value,
        w_out,
    )
    return (features_t.T, (normed * out_gain).astype(BF16))


def solution(mesh):
    n_sn = mesh.shape["sn"]
    owners = mesh.shape["pts"] * n_sn
    everything = ("groups", "pts", "sn")
    in_specs = (
        P(everything, None),
        P(None, everything),
        P(None, everything),
        P(),
        P("groups"),
        P(everything, None),
        P("groups"),
        P("groups"),
        P(),
        P(),
        P(),
        P(),
        P(),
        P(),
        P(),
    )
    out_specs = (P(everything, None), P(everything, None))
    return jax.shard_map(
        functools.partial(per_device, n_sn, owners),
        mesh=mesh,
        in_specs=in_specs,
        out_specs=out_specs,
        check_vma=False,
    )
```
